512 devices in a mesh: dp: 8 (over y), expert: 64 (over x, z, core).
Axes of the slice: x: 4, y: 8, z: 8, core: 2. Of those that a mesh axis runs over, the one named last changes fastest.
Arguments:
- tokens: bfloat16 [8192, 3584], P('expert', 'dp'), may hold values from -6 to 6
- cotangent: bfloat16 [8192, 3584], P('expert', 'dp'), may hold values from -12 to 12
- expert_ids: int32 [8192, 8], P('expert'), may hold values from 0 to 63, all different within a row; in each aligned block of 128 rows (0 to 127, 128 to 255, ...) at most 16 rows name the same one
- gate_levels: int32 [8192, 8], P('expert'), may hold values from 1 to 15
- capacity: int32 [64], replicated, may hold values from 4 to 16, as said below
- up_weight: bfloat16 [64, 3584, 1024], P('expert', 'dp'), may hold values from -0.09375 to 0.09375
- down_weight: bfloat16 [64, 3584, 1024], P('expert', 'dp'), may hold values from -0.1875 to 0.1875
Outputs:
- token_grad: bfloat16 [8192, 3584], P('expert', 'dp')
- up_grad: bfloat16 [64, 3584, 1024], P('expert', 'dp')
- down_grad: bfloat16 [64, 3584, 1024], P('expert', 'dp')
The draws below stay inside these ranges and needn't reach their ends.
Inputs may be any that keep to these rules, and one draw needn't show every extreme that they name: `expert_ids`: in each aligned block of 128 tokens every expert is named by exactly 16 choices. `capacity`: some expert accepts 16 rows and some only 4.
All inputs are finite; a program needn't handle non-finite values.
Results may differ from the reference program's by a relative error of at most 0.023.
Values may be sent and summed in bfloat16 or wider, within the bound.
A program may use at most 64 MiB of HBM per device.

```python
import math
import jax
import jax.numpy as jnp
import numpy as np
from jax import lax

D = 3584
HW = 1024
TOP = 8
TOK_DEV = 128
EXPERTS = 64
TOKENS = 8192
CAP = 16
N_DP = 8
N_EXPERT = 64


def draw_capacity(key, part):
    least = (CAP + 3) // 4
    values = jax.random.randint(key, (EXPERTS,), least, CAP + 1)
    order = jax.random.permutation(jax.random.fold_in(key, 7), EXPERTS)
    values = values.at[order[0]].set(CAP)
    values = values.at[order[1]].set(least)
    return values.astype(jnp.int32)


def with_ends(array, rng, low, top_value):
    index_at = [jax.random.randint(jax.random.fold_in(rng, axis), (), 0, length) for axis, length in enumerate(array.shape)]
    longest = array.shape.index(max(array.shape))
    next_to = index_at[:longest] + [(index_at[longest] + 1) % array.shape[longest]] + index_at[longest + 1:]
    return array.at[tuple(index_at)].set(low).at[tuple(next_to)].set(top_value)


def level_of(key, extent, shards, smallest, high):
    factor_of, own = 1.0, jax.random.fold_in(key, 6)
    for dim, parts in shards:
        heights = jnp.exp(jax.random.uniform(jax.random.fold_in(own, dim), (parts,), jnp.float32, smallest / len(shards), high / len(shards)))
        factor_of = factor_of * jnp.repeat(heights, extent[dim] // parts).reshape([-1 if axis == dim else 1 for axis in range(len(extent))])
    return factor_of


def assign_block(stream_key, own, number, rows, count, top, most, skew):
    sequence = jax.random.permutation(stream_key, count)
    packed, common = shares(count, rows * top, most, skew, True), shares(count, rows * top, most, skew, False)
    places = jnp.arange(count)

    def named(sizes, offset_by):
        used = int((sizes > 0).sum())
        fixed = max(1, used // 4)
        moved = fixed + (places - fixed + offset_by * (used - fixed)) % max(1, count - fixed)
        return jnp.zeros((count,), jnp.int32).at[sequence[jnp.where(places < fixed, places, moved)]].set(jnp.asarray(sizes, jnp.int32))

    sizes = jnp.where(number % 4 == 0, named(packed, number // 4), named(common, number - number // 4 - 1))
    mixed = jax.random.permutation(jax.random.fold_in(own, 3), count)
    source_of, receiver = mixed[0:count // 2 * 2:2], mixed[1:count // 2 * 2:2]
    margin = jnp.minimum(sizes[source_of] - 1, most - sizes[receiver]) // 2
    margin = jnp.where((source_of == sequence[0]) | (receiver == sequence[0]) | (sizes[receiver] == 0), 0, jnp.maximum(margin, 0))
    moved = jax.random.randint(jax.random.fold_in(own, 4), (count // 2,), 0, 1 << 20) % (margin + 1)
    sizes = sizes.at[source_of].add(-moved).at[receiver].add(moved)
    items = jnp.searchsorted(jnp.cumsum(sizes), jnp.arange(rows * top), side="right").astype(jnp.int32)
    grid = items.reshape(top, rows).T
    grid = grid[jax.random.permutation(jax.random.fold_in(own, 1), rows)]
    offset_by = jax.random.randint(jax.random.fold_in(own, 2), (rows, 1), 0, top)
    return jnp.take_along_axis(grid, (jnp.arange(top)[None, :] + offset_by) % top, axis=1)


def shares(count, total, bound, skew, full):
    weights = [(1 << 20) // math.isqrt(grade ** skew) + 1 for grade in range(1, count + 1)]
    largest = bound if full else min(bound, max(-(-total // count), total * weights[0] // sum(weights)))
    least = 1 if total - largest >= count - 1 else 0
    counts, surplus = [largest] + [least] * (count - 1), total - largest - least * (count - 1)
    while surplus > 0:
        movable = [i for i in range(1, count) if counts[i] < largest] or [i for i in range(1, count) if counts[i] < bound]
        whole, remaining = sum([weights[i] for i in movable]), surplus
        for i in movable:
            addition = min(bound - counts[i], max(1, remaining * weights[i] // whole), surplus)
            counts[i] = counts[i] + addition
            surplus = surplus - addition
    return np.array(counts)


def bell_draw(stream_key, extent, scale, most, cuts=(), kind=jnp.bfloat16):
    entries = jax.random.normal(stream_key, extent, jnp.float32) * scale
    if len(cuts) > 0:
        entries = level_of(stream_key, extent, cuts, -0.22, 0.18) * entries
    return jnp.clip(entries, min=-most, max=most).astype(kind)


def setup_inputs(seed: int = 0) -> dict:
    keys = jax.random.split(jax.random.key(seed), 8)
    tokens = bell_draw(keys[0], (TOKENS, D), 1.0, 6.0, ((0, 64), (1, 8)))
    cotangent = bell_draw(keys[1], (TOKENS, D), 2.0, 12.0, ((0, 64), (1, 8)))
    expert_ids_keys = jax.random.split(jax.random.fold_in(keys[2], 1), TOKENS // TOK_DEV)
    expert_ids_turns = jax.random.permutation(jax.random.fold_in(keys[2], 3), TOKENS // TOK_DEV)
    expert_ids = jax.vmap(lambda own, number: assign_block(jax.random.fold_in(keys[2], 2), own, number, TOK_DEV, EXPERTS, TOP, CAP, 0))(expert_ids_keys, expert_ids_turns).reshape((TOKENS, TOP))
    gate_levels = with_ends(jax.random.randint(keys[3], (TOKENS, TOP), 1, 16), jax.random.fold_in(keys[3], 1), 1, 15).astype(jnp.int32)
    capacity = draw_capacity(jax.random.fold_in(keys[7], 71), 0)
    up_weight = bell_draw(keys[5], (EXPERTS, D, HW), D ** -0.5, 0.09375, ((0, 64), (1, 8)))
    down_weight = bell_draw(keys[6], (EXPERTS, D, HW), HW ** -0.5, 0.1875, ((0, 64), (1, 8)))
    return dict(tokens=tokens, cotangent=cotangent, expert_ids=expert_ids, gate_levels=gate_levels, capacity=capacity, up_weight=up_weight, down_weight=down_weight)


def silu_slope(preact):
    sigmoid = jax.nn.sigmoid(preact)
    return sigmoid * (1.0 + preact * (1.0 - sigmoid))


def grouped_partials(rows, weight):
    row_count = rows.shape[0]
    group_width = weight.shape[0] // N_DP
    rows_split = rows.astype(jnp.float32).reshape(row_count, N_DP, group_width)
    weight_split = weight.astype(jnp.float32).reshape(N_DP, group_width, weight.shape[1])
    partials = jnp.einsum('rpd,pdh->prh', rows_split, weight_split)
    rounded = lax.optimization_barrier(partials.astype(jnp.bfloat16))
    return jnp.sum(rounded.astype(jnp.float32), axis=0)


def reference(tokens, cotangent, expert_ids, gate_levels, capacity, up_weight, down_weight):
    num_blocks = N_EXPERT
    block_routes = TOK_DEV * TOP
    ids_blocks = expert_ids.reshape(num_blocks, block_routes)
    experts_row = jnp.arange(EXPERTS, dtype=jnp.int32)
    onehot = (ids_blocks[:, :, None] == experts_row[None, None, :]).astype(jnp.int32)
    earlier = jnp.cumsum(onehot, axis=1) - onehot
    slot_rank = jnp.sum(earlier * onehot, axis=2).astype(jnp.int32)
    kept_mask = (slot_rank < capacity[ids_blocks]).astype(jnp.int32)
    block_index = jnp.broadcast_to(jnp.arange(num_blocks, dtype=jnp.int32)[:, None], (num_blocks, block_routes))
    route_index = jnp.arange(num_blocks * block_routes, dtype=jnp.int32).reshape(num_blocks, block_routes)
    route_table = jnp.zeros((EXPERTS, num_blocks, CAP), jnp.int32).at[ids_blocks, block_index, slot_rank].set(route_index)
    mask_table = jnp.zeros((EXPERTS, num_blocks, CAP), jnp.int32).at[ids_blocks, block_index, slot_rank].set(kept_mask)
    levels = gate_levels.astype(jnp.float32)
    gate_weights = (levels / jnp.sum(levels, axis=1, keepdims=True)).reshape(-1)

    def per_expert(running, expert):
        routes = route_table[expert].reshape(-1)
        keep_rows = mask_table[expert].reshape(-1).astype(jnp.float32)
        token_index = (routes // TOP).astype(jnp.int32)
        expert_in = (tokens[token_index].astype(jnp.float32) * keep_rows[:, None]).astype(jnp.bfloat16)
        scaled = (gate_weights[routes][:, None] * cotangent[token_index].astype(jnp.float32)).astype(jnp.bfloat16)
        expert_cot = (scaled.astype(jnp.float32) * keep_rows[:, None]).astype(jnp.bfloat16)
        weight_up = up_weight[expert]
        weight_down = down_weight[expert]
        preact = grouped_partials(expert_in, weight_up)
        hidden_cot = grouped_partials(expert_cot, weight_down)
        hidden = jax.nn.silu(preact).astype(jnp.bfloat16)
        act_cot = (hidden_cot * silu_slope(preact)).astype(jnp.bfloat16)
        in_f32 = expert_in.astype(jnp.float32)
        cot_f32 = expert_cot.astype(jnp.float32)
        act_f32 = act_cot.astype(jnp.float32)
        grad_up = jnp.dot(in_f32.T, act_f32).astype(jnp.bfloat16)
        grad_down = jnp.dot(cot_f32.T, hidden.astype(jnp.float32)).astype(jnp.bfloat16)
        row_grad = jnp.dot(act_f32, weight_up.astype(jnp.float32).T).astype(jnp.bfloat16)
        running = running.at[token_index].add(row_grad.astype(jnp.float32))
        return running, (grad_up, grad_down)

    start_grad = jnp.zeros((TOKENS, D), jnp.float32)
    summed, grads = lax.scan(per_expert, start_grad, jnp.arange(EXPERTS, dtype=jnp.int32))
    return summed.astype(jnp.bfloat16), grads[0], grads[1]
```

```python
import functools

import jax
import jax.numpy as jnp
from jax import lax
from jax.experimental import pallas as pl
from jax.experimental.pallas import tpu as pltpu
from jax.sharding import PartitionSpec as P

MESH = pl.DeviceIdType.MESH
NN = (((1,), (0,)), ((), ()))
NT = (((1,), (1,)), ((), ()))
TN = (((0,), (0,)), ((), ()))
SPACING = 4


def matmul(left, right, dims=NN):
    return lax.dot_general(left, right, dims, preferred_element_type=jnp.float32)


def layer_kernel(
    groups,
    members,
    ring,
    slots,
    tokens_ref,
    cot_ref,
    ids_ref,
    levels_ref,
    capacity_ref,
    up_hbm,
    down_hbm,
    token_grad_ref,
    up_grad_hbm,
    down_grad_hbm,
    send_ref,
    recv_ref,
    recv_turned,
    placing_ref,
    rank_ref,
    level_ref,
    up_ref,
    down_ref,
    part_ref,
    sums_ref,
    full_ref,
    back_ref,
    returned_ref,
    combined_ref,
    up_grad_ref,
    down_grad_ref,
    local_sem,
    out_send,
    out_recv,
    sum_send,
    sum_recv,
    full_send,
    full_recv,
    back_send,
    back_recv,
):
    experts = groups * members
    width, tok_rows = tokens_ref.shape
    hidden = up_ref.shape[1]
    piece = hidden // ring
    depth = up_ref.shape[0]
    chunk = members * slots
    top = ids_ref.shape[0]
    me_dp = lax.axis_index("dp")
    me = lax.axis_index("expert")
    my_group = lax.div(me, members)
    my_member = lax.rem(me, members)
    after = lax.rem(me_dp + 1, ring)
    before = lax.rem(me_dp + ring - 1, ring)
    longest = ring // 2

    def reach(matrix, direction):
        far = matrix == direction
        return longest if far else ring - 1 - longest

    def hop_slot(matrix, direction, hop):
        return (hop - 1) if direction == 0 else reach(matrix, 0) + hop - 1

    def neighbour(direction):
        return {"dp": after if direction == 0 else before}

    def ring_index(offset):
        return lax.rem(me_dp + offset + ring, ring)

    barrier = pltpu.get_barrier_semaphore()

    def greet(step, carry):
        pl.semaphore_signal(
            barrier,
            inc=1,
            device_id={"expert": lax.rem(me + step, experts)},
            device_id_type=MESH,
        )
        return carry

    lax.fori_loop(1, experts, greet, 0)
    for direction in range(2):
        pl.semaphore_signal(barrier, inc=1, device_id=neighbour(direction), device_id_type=MESH)

    up_rows = pl.ds(0, width)
    down_rows = pl.ds(depth - width, width)
    load_up = pltpu.make_async_copy(up_hbm, up_ref.at[up_rows], local_sem.at[0])
    load_down = pltpu.make_async_copy(down_hbm, down_ref.at[down_rows], local_sem.at[1])
    load_up.start()
    load_down.start()
    up_ref[pl.ds(width, depth - width), :] = jnp.zeros((depth - width, hidden), jnp.bfloat16)
    down_ref[pl.ds(0, depth - width), :] = jnp.zeros((depth - width, hidden), jnp.bfloat16)

    ids = ids_ref[...]
    levels = levels_ref[...]
    expert_row = lax.broadcasted_iota(jnp.int32, (experts, tok_rows), 0)
    named = jnp.zeros((experts, tok_rows), jnp.float32)
    level = jnp.zeros((experts, tok_rows), jnp.float32)
    for choice in range(top):
        hit = ids[choice : choice + 1, :] == expert_row
        named = named + jnp.where(hit, 1.0, 0.0)
        level = level + jnp.where(hit, levels[choice : choice + 1, :].astype(jnp.float32), 0.0)
    total = jnp.sum(levels.astype(jnp.float32), axis=0, keepdims=True)
    earlier = lax.broadcasted_iota(jnp.int32, (tok_rows, tok_rows), 0) < lax.broadcasted_iota(
        jnp.int32, (tok_rows, tok_rows), 1
    )
    rank = matmul(named.astype(jnp.bfloat16), jnp.where(earlier, 1.0, 0.0).astype(jnp.bfloat16))
    diagonal = lax.broadcasted_iota(jnp.int32, (experts, experts), 0) == lax.broadcasted_iota(
        jnp.int32, (experts, experts), 1
    )
    limit = jnp.sum(
        jnp.where(diagonal, capacity_ref[...].astype(jnp.float32), 0.0), axis=1, keepdims=True
    )
    kept = (named > 0.0) & (rank < limit)
    rank_ref[...] = jnp.where(kept, rank, -1.0).astype(jnp.bfloat16)
    level_ref[...] = level.astype(jnp.bfloat16)

    def out_base(step):
        return pl.multiple_of(lax.rem(my_group + step, groups) * chunk, chunk)

    def place(step):
        base = out_base(step)
        row = base + lax.broadcasted_iota(jnp.int32, (chunk, experts), 0)
        column = lax.broadcasted_iota(jnp.int32, (chunk, experts), 1)
        mine = lax.div(row, slots) == column
        spread = jnp.where(mine, 1.0, 0.0).astype(jnp.bfloat16)
        slot = lax.rem(lax.broadcasted_iota(jnp.int32, (chunk, tok_rows), 0), slots)
        matched = matmul(spread, rank_ref[...]) == slot.astype(jnp.float32)
        placing = jnp.where(matched, 1.0, 0.0)
        slot_level = jnp.sum(placing * matmul(spread, level_ref[...]), axis=1, keepdims=True)
        slot_total = jnp.sum(placing * total, axis=1, keepdims=True)
        gate = jnp.where(slot_total > 0.0, slot_level / jnp.maximum(slot_total, 1.0), 0.0)
        placing = placing.astype(jnp.bfloat16)
        placing_ref[pl.ds(base, chunk), :] = placing
        both = jnp.concatenate([tokens_ref[...], cot_ref[...]], axis=0)
        rows = matmul(placing, both, NT)
        in_cot = lax.broadcasted_iota(jnp.int32, (chunk, 2 * width), 1) >= width
        rows = jnp.where(in_cot, gate * rows, rows)
        send_ref[pl.ds(base, chunk), :] = rows.astype(jnp.bfloat16)
        if step == 0:
            own = pl.multiple_of(me * slots, slots)
            to = pl.multiple_of(my_member * slots, slots)
            recv_ref[pl.ds(to, slots), :] = send_ref[pl.ds(own, slots), :]

    def send_out(step):
        group = lax.rem(my_group + step, groups)

        def one(index, carry):
            peer = group * members + lax.rem(my_member + index, members)
            pltpu.make_async_remote_copy(
                src_ref=send_ref.at[pl.ds(pl.multiple_of(peer * slots, slots), slots)],
                dst_ref=recv_ref.at[
                    pl.ds(pl.multiple_of(step * chunk + my_member * slots, slots), slots)
                ],
                send_sem=out_send,
                recv_sem=out_recv.at[step],
                device_id={"expert": peer},
                device_id_type=MESH,
            ).start()
            return carry

        lax.fori_loop(1 if step == 0 else 0, members, one, 0)

    def wait_for(ref, sem):
        pltpu.make_async_copy(ref, ref, sem).wait()

    def chunk_rows(step):
        return pl.ds(step * chunk, chunk)

    def arrived_rows(step):
        return pl.ds(0, chunk - slots if step == 0 else chunk)

    def ring_copy(source, target, send_sem, recv_sem, direction):
        pltpu.make_async_remote_copy(
            src_ref=source,
            dst_ref=target,
            send_sem=send_sem,
            recv_sem=recv_sem,
            device_id=neighbour(direction),
            device_id_type=MESH,
        ).start()

    routes = [(matrix, direction) for matrix in range(2) for direction in range(2)]

    def sum_hop(step, matrix, direction, hop):
        offset = reach(matrix, direction) - hop + 1
        owner = ring_index(offset if direction == 0 else -offset)
        slot = hop_slot(matrix, direction, hop)
        if hop > 1:
            came = hop_slot(matrix, direction, hop - 1)
            wait_for(sums_ref.at[step, matrix, came], sum_recv.at[step, matrix, came])
            part_ref[step, matrix, owner] = (
                part_ref[step, matrix, owner].astype(jnp.float32)
                + sums_ref[step, matrix, came].astype(jnp.float32)
            ).astype(jnp.bfloat16)
        ring_copy(
            part_ref.at[step, matrix, owner],
            sums_ref.at[step, matrix, slot],
            sum_send,
            sum_recv.at[step, matrix, slot],
            direction,
        )

    def summed(step, matrix):
        value = part_ref[step, matrix, me_dp].astype(jnp.float32)
        for direction in range(2):
            came = hop_slot(matrix, direction, reach(matrix, direction))
            wait_for(sums_ref.at[step, matrix, came], sum_recv.at[step, matrix, came])
            value = value + sums_ref[step, matrix, came].astype(jnp.float32)
        return value

    def full_wait(step, matrix, direction, hop):
        owner = ring_index(-hop if direction == 0 else hop)
        came = hop_slot(matrix, direction, hop)
        wait_for(full_ref.at[step, matrix, owner], full_recv.at[step, matrix, came])

    def full_hop(step, matrix, direction, hop):
        offset = hop - 1
        owner = ring_index(-offset if direction == 0 else offset)
        if hop > 1:
            full_wait(step, matrix, direction, hop - 1)
        slot = hop_slot(matrix, direction, hop)
        ring_copy(
            full_ref.at[step, matrix, owner],
            full_ref.at[step, matrix, owner],
            full_send,
            full_recv.at[step, matrix, slot],
            direction,
        )

    def forward(step):
        wait_for(recv_ref.at[arrived_rows(step)], out_recv.at[step])
        if step == 0:
            load_up.wait()
            load_down.wait()
        for matrix in range(2):
            weight = up_ref if matrix == 0 else down_ref
            start = 0 if matrix == 0 else 2 * width - depth

            def columns(block, carry, matrix=matrix, weight=weight, start=start):
                where = pl.ds(pl.multiple_of(block * 2 * piece, 2 * piece), 2 * piece)
                terms = matmul(recv_ref[chunk_rows(step), start : start + depth], weight[:, where])
                terms = terms.astype(jnp.bfloat16)
                part_ref[step, matrix, 2 * block] = terms[:, :piece]
                part_ref[step, matrix, 2 * block + 1] = terms[:, piece:]
                return carry

            lax.fori_loop(0, ring // 2, columns, 0)
        for matrix, direction in routes:
            sum_hop(step, matrix, direction, 1)

    def turn(step):
        recv_turned[:, chunk_rows(step)] = recv_ref[chunk_rows(step), :].T

    def activate(step):
        preact = summed(step, 0)
        sigmoid = jax.nn.sigmoid(preact)
        full_ref[step, 0, me_dp] = (preact * sigmoid).astype(jnp.bfloat16)
        for direction in range(2):
            full_hop(step, 0, direction, 1)
        slope = sigmoid * (1.0 + preact * (1.0 - sigmoid))
        full_ref[step, 1, me_dp] = (summed(step, 1) * slope).astype(jnp.bfloat16)
        for direction in range(2):
            full_hop(step, 1, direction, 1)

    def backward(step):
        for direction in range(2):
            full_wait(step, 1, direction, reach(1, direction))
        act_cot = jnp.concatenate([full_ref[step, 1, index] for index in range(ring)], axis=1)
        rows = matmul(act_cot, up_ref[...], NT)
        back_ref[chunk_rows(step), :] = rows[:, :width].astype(jnp.bfloat16)
        own = pl.multiple_of(me * slots, slots)
        if step == 0:
            at = pl.multiple_of(my_member * slots, slots)
            returned_ref[pl.ds(own, slots), :] = back_ref[pl.ds(at, slots), :]
        group = lax.rem(my_group + groups - step, groups)

        def one(index, carry):
            member = lax.rem(my_member + index, members)
            pltpu.make_async_remote_copy(
                src_ref=back_ref.at[
                    pl.ds(pl.multiple_of(step * chunk + member * slots, slots), slots)
                ],
                dst_ref=returned_ref.at[pl.ds(own, slots)],
                send_sem=back_send,
                recv_sem=back_recv.at[step],
                device_id={"expert": group * members + member},
                device_id_type=MESH,
            ).start()
            return carry

        lax.fori_loop(1 if step == 0 else 0, members, one, 0)
        for direction in range(2):
            full_wait(step, 0, direction, reach(0, direction))

    def combine(step):
        wait_for(returned_ref.at[arrived_rows(step)], back_recv.at[step])
        base = out_base(step)
        rows = pl.ds(base, chunk)
        terms = matmul(placing_ref[rows, :], returned_ref[rows, :], TN)
        combined_ref[...] = terms if step == 0 else combined_ref[...] + terms

    def weight_grads():
        def columns(block, carry):
            where = pl.ds(pl.multiple_of(block * 2 * piece, 2 * piece), 2 * piece)

            def pieces(matrix):
                return jnp.concatenate(
                    [
                        jnp.concatenate(
                            [full_ref[step, matrix, 2 * block + half] for half in range(2)], axis=1
                        )
                        for step in range(groups)
                    ],
                    axis=0,
                )

            up_grad_ref[:, where] = matmul(recv_turned[:width, :], pieces(1)).astype(jnp.bfloat16)
            down_grad_ref[:, where] = matmul(recv_turned[width:, :], pieces(0)).astype(jnp.bfloat16)
            return carry

        lax.fori_loop(0, ring // 2, columns, 0)

    place(0)
    pl.semaphore_wait(barrier, experts + 1)
    send_out(0)
    for step in range(1, groups):
        place(step)
        send_out(step)

    def stage(step, number):
        if number == 0:
            forward(step)
        elif number < longest:
            for matrix, direction in routes:
                if number + 1 <= reach(matrix, direction):
                    sum_hop(step, matrix, direction, number + 1)
            if number == 1:
                turn(step)
        elif number == longest:
            activate(step)
        elif number < 2 * longest:
            for matrix, direction in routes:
                if number - longest + 1 <= reach(matrix, direction):
                    full_hop(step, matrix, direction, number - longest + 1)
        elif number == 2 * longest:
            backward(step)

    for tick in range((groups - 1) * SPACING + 2 * longest + 1):
        for step in range(groups):
            if 0 <= tick - step * SPACING <= 2 * longest:
                stage(step, tick - step * SPACING)

    weight_grads()
    store_up = pltpu.make_async_copy(up_grad_ref, up_grad_hbm, local_sem.at[0])
    store_down = pltpu.make_async_copy(down_grad_ref, down_grad_hbm, local_sem.at[1])
    store_up.start()
    store_down.start()
    for step in range(groups):
        combine(step)
    token_grad_ref[...] = combined_ref[...].T.astype(jnp.bfloat16)

    moved = pl.ds(0, experts * slots - slots)
    wait_for(send_ref.at[moved], out_send)
    wait_for(back_ref.at[moved], back_send)
    wait_for(part_ref.at[:, :, pl.ds(0, ring - 1)], sum_send)
    wait_for(full_ref.at[:, :, pl.ds(0, ring - 1)], full_send)
    store_up.wait()
    store_down.wait()


def per_device(
    groups, members, ring, tokens, cotangent, expert_ids, gate_levels, capacity, up_weight, down_weight
):
    tok_rows, width = tokens.shape
    experts = groups * members
    slots = tok_rows * expert_ids.shape[1] // experts
    rows = experts * slots
    chunk = members * slots
    hidden = up_weight.shape[2]
    piece = hidden // ring
    depth = -(-width // 128) * 128
    half = jnp.bfloat16
    vmem = pl.BlockSpec(memory_space=pltpu.VMEM)
    anywhere = pl.BlockSpec(memory_space=pl.ANY)
    dma = pltpu.SemaphoreType.DMA
    token_grad, up_grad, down_grad = pl.pallas_call(
        functools.partial(layer_kernel, groups, members, ring, slots),
        out_shape=(
            jax.ShapeDtypeStruct((width, tok_rows), half),
            jax.ShapeDtypeStruct((width, hidden), half),
            jax.ShapeDtypeStruct((width, hidden), half),
        ),
        in_specs=[vmem] * 5 + [anywhere] * 2,
        out_specs=(vmem, anywhere, anywhere),
        scratch_shapes=[
            pltpu.VMEM((rows, 2 * width), half),
            pltpu.VMEM((rows, 2 * width), half),
            pltpu.VMEM((2 * width, rows), half),
            pltpu.VMEM((rows, tok_rows), half),
            pltpu.VMEM((experts, tok_rows), half),
            pltpu.VMEM((experts, tok_rows), half),
            pltpu.VMEM((depth, hidden), half),
            pltpu.VMEM((depth, hidden), half),
            pltpu.VMEM((groups, 2, ring, chunk, piece), half),
            pltpu.VMEM((groups, 2, ring - 1, chunk, piece), half),
            pltpu.VMEM((groups, 2, ring, chunk, piece), half),
            pltpu.VMEM((rows, width), half),
            pltpu.VMEM((rows, width), half),
            pltpu.VMEM((tok_rows, width), jnp.float32),
            pltpu.VMEM((width, hidden), half),
            pltpu.VMEM((width, hidden), half),
            dma((2,)),
            dma,
            dma((groups,)),
            dma,
            dma((groups, 2, ring - 1)),
            dma,
            dma((groups, 2, ring - 1)),
            dma,
            dma((groups,)),
        ],
        compiler_params=pltpu.CompilerParams(
            collective_id=0, has_side_effects=True, vmem_limit_bytes=56 * 1024 * 1024
        ),
    )(
        tokens.T,
        cotangent.T,
        expert_ids.T,
        gate_levels.T,
        capacity.reshape(1, experts),
        up_weight[0],
        down_weight[0],
    )
    return token_grad.T, up_grad[None], down_grad[None]


def solution(mesh):
    ring, experts = mesh.shape["dp"], mesh.shape["expert"]
    groups = 4
    return jax.shard_map(
        functools.partial(per_device, groups, experts // groups, ring),
        mesh=mesh,
        in_specs=(
            P("expert", "dp"),
            P("expert", "dp"),
            P("expert", None),
            P("expert", None),
            P(),
            P("expert", "dp", None),
            P("expert", "dp", None),
        ),
        out_specs=(P("expert", "dp"), P("expert", "dp", None), P("expert", "dp", None)),
        check_vma=False,
    )
```

```python
import functools

import jax
import jax.numpy as jnp
from jax import lax
from jax.experimental import pallas as pl
from jax.experimental.pallas import tpu as pltpu
from jax.sharding import PartitionSpec as P

MESH = pl.DeviceIdType.MESH
NN = (((1,), (0,)), ((), ()))
NT = (((1,), (1,)), ((), ()))
TN = (((0,), (0,)), ((), ()))
CHUNKS = 8
STARTS = {2: (0, 3), 4: (0, 4, 7, 9), 8: (0, 1, 2, 4, 6, 8, 10, 11)}
X_CHIPS, CORES = 4, 2
CHUNK_ORDER = {1: (0,), 2: (0, 1), 4: (0, 2, 3, 1), 8: (0, 1, 4, 6, 7, 5, 3, 2)}


def matmul(left, right, dims=NN):
    return lax.dot_general(left, right, dims, preferred_element_type=jnp.float32)


def layer_kernel(
    chunks,
    z_chips,
    ring,
    slots,
    tokens_ref,
    cot_ref,
    ids_ref,
    levels_ref,
    capacity_ref,
    up_hbm,
    down_hbm,
    token_grad_ref,
    up_grad_hbm,
    down_grad_hbm,
    send_ref,
    recv_ref,
    recv_turned,
    placing_ref,
    rank_ref,
    level_ref,
    up_ref,
    down_ref,
    part_ref,
    sums_ref,
    full_ref,
    back_ref,
    returned_ref,
    combined_ref,
    grad_sums_ref,
    up_grad_ref,
    down_grad_ref,
    local_sem,
    out_send,
    out_recv,
    sum_send,
    sum_recv,
    full_send,
    full_recv,
    back_send,
    back_recv,
):
    experts = X_CHIPS * z_chips * CORES
    width, tok_rows = tokens_ref.shape
    hidden = up_ref.shape[1]
    piece = hidden // ring
    depth = up_ref.shape[0]
    distances = z_chips // chunks
    layer = X_CHIPS * CORES * slots
    chunk = distances * layer
    top = ids_ref.shape[0]
    me_dp = lax.axis_index("dp")
    me = lax.axis_index("expert")
    my_core = lax.rem(me, CORES)
    my_z = lax.rem(lax.div(me, CORES), z_chips)
    my_x = lax.div(me, CORES * z_chips)
    after = lax.rem(me_dp + 1, ring)
    before = lax.rem(me_dp + ring - 1, ring)
    longest = ring // 2

    def distance(step, index):
        number = CHUNK_ORDER[chunks][step] * distances + index
        return (number + 1) // 2 * (1 if number % 2 else -1)

    def reach(matrix, direction):
        far = matrix == direction
        return longest if far else ring - 1 - longest

    def hop_slot(matrix, direction, hop):
        return (hop - 1) if direction == 0 else reach(matrix, 0) + hop - 1

    def neighbour(direction):
        return {"dp": after if direction == 0 else before}

    def ring_index(offset):
        return lax.rem(me_dp + offset + ring, ring)

    barrier = pltpu.get_barrier_semaphore()

    def greet(step, carry):
        pl.semaphore_signal(
            barrier,
            inc=1,
            device_id={"expert": lax.rem(me + step, experts)},
            device_id_type=MESH,
        )
        return carry

    lax.fori_loop(1, experts, greet, 0)
    for direction in range(2):
        pl.semaphore_signal(barrier, inc=1, device_id=neighbour(direction), device_id_type=MESH)

    up_rows = pl.ds(0, width)
    down_rows = pl.ds(depth - width, width)
    load_up = pltpu.make_async_copy(up_hbm, up_ref.at[up_rows], local_sem.at[0])
    load_down = pltpu.make_async_copy(down_hbm, down_ref.at[down_rows], local_sem.at[1])
    load_up.start()
    load_down.start()
    up_ref[pl.ds(width, depth - width), :] = jnp.zeros((depth - width, hidden), jnp.bfloat16)
    down_ref[pl.ds(0, depth - width), :] = jnp.zeros((depth - width, hidden), jnp.bfloat16)

    ids = ids_ref[...]
    levels = levels_ref[...]
    expert_row = lax.broadcasted_iota(jnp.int32, (experts, tok_rows), 0)
    named = jnp.zeros((experts, tok_rows), jnp.float32)
    level = jnp.zeros((experts, tok_rows), jnp.float32)
    for choice in range(top):
        hit = ids[choice : choice + 1, :] == expert_row
        named = named + jnp.where(hit, 1.0, 0.0)
        level = level + jnp.where(hit, levels[choice : choice + 1, :].astype(jnp.float32), 0.0)
    total = jnp.sum(levels.astype(jnp.float32), axis=0, keepdims=True)
    earlier = lax.broadcasted_iota(jnp.int32, (tok_rows, tok_rows), 0) < lax.broadcasted_iota(
        jnp.int32, (tok_rows, tok_rows), 1
    )
    rank = matmul(named.astype(jnp.bfloat16), jnp.where(earlier, 1.0, 0.0).astype(jnp.bfloat16))
    diagonal = lax.broadcasted_iota(jnp.int32, (experts, experts), 0) == lax.broadcasted_iota(
        jnp.int32, (experts, experts), 1
    )
    limit = jnp.sum(
        jnp.where(diagonal, capacity_ref[...].astype(jnp.float32), 0.0), axis=1, keepdims=True
    )
    kept = (named > 0.0) & (rank < limit)
    rank_ref[...] = jnp.where(kept, rank, -1.0).astype(jnp.bfloat16)
    level_ref[...] = level.astype(jnp.bfloat16)

    def chunk_rows(step):
        return pl.ds(step * chunk, chunk)

    def place(step):
        row = lax.broadcasted_iota(jnp.int32, (chunk, 1), 0)
        core = (row >> (slots.bit_length() - 1)) & (CORES - 1)
        x_away = (row >> ((CORES * slots).bit_length() - 1)) & (X_CHIPS - 1)
        z_away = jnp.zeros((chunk, 1), jnp.int32)
        for index in range(distances):
            here = (row >> (layer.bit_length() - 1)) == index
            z_away = jnp.where(here, distance(step, index), z_away)
        z_away = jnp.where((x_away & 1) == 1, -z_away, z_away)
        x_to = (my_x + x_away) & (X_CHIPS - 1)
        z_to = (my_z + z_away) & (z_chips - 1)
        expert = (x_to * z_chips + z_to) * CORES + core
        mine = expert == lax.broadcasted_iota(jnp.int32, (chunk, experts), 1)
        spread = jnp.where(mine, 1.0, 0.0).astype(jnp.bfloat16)
        slot = lax.broadcasted_iota(jnp.int32, (chunk, tok_rows), 0) & (slots - 1)
        matched = matmul(spread, rank_ref[...]) == slot.astype(jnp.float32)
        placing = jnp.where(matched, 1.0, 0.0)
        slot_level = jnp.sum(placing * matmul(spread, level_ref[...]), axis=1, keepdims=True)
        slot_total = jnp.sum(placing * total, axis=1, keepdims=True)
        gate = jnp.where(slot_total > 0.0, slot_level / jnp.maximum(slot_total, 1.0), 0.0)
        placing = placing.astype(jnp.bfloat16)
        placing_ref[chunk_rows(step), :] = placing
        both = jnp.concatenate([tokens_ref[...], cot_ref[...]], axis=0)
        rows = matmul(placing, both, NT)
        in_cot = lax.broadcasted_iota(jnp.int32, (chunk, 2 * width), 1) >= width
        rows = jnp.where(in_cot, gate * rows, rows)
        send_ref[chunk_rows(step), :] = rows.astype(jnp.bfloat16)
        if step == 0:
            own = pl.ds(pl.multiple_of(my_core * slots, slots), slots)
            recv_ref[own, :] = send_ref[own, :]

    def exchange(step, side, source, target, send_sem, recv_sem):
        for index in range(distances):
            base = step * chunk + index * layer

            def one(turn, carry, index=index, base=base):
                x_away = lax.div(turn, CORES)
                core = lax.rem(my_core + turn, CORES)
                z_away = distance(step, index) * (1 - 2 * lax.rem(x_away, 2))
                x_to = lax.rem(my_x + side * x_away + X_CHIPS, X_CHIPS)
                z_to = lax.rem(my_z + side * z_away + z_chips, z_chips)
                place_from = base + (x_away * CORES + core) * slots
                place_to = base + (x_away * CORES + my_core) * slots
                pltpu.make_async_remote_copy(
                    src_ref=source.at[pl.ds(pl.multiple_of(place_from, slots), slots)],
                    dst_ref=target.at[pl.ds(pl.multiple_of(place_to, slots), slots)],
                    send_sem=send_sem,
                    recv_sem=recv_sem.at[step],
                    device_id={"expert": (x_to * z_chips + z_to) * CORES + core},
                    device_id_type=MESH,
                ).start()
                return carry

            own = step == 0 and index == 0
            lax.fori_loop(1 if own else 0, X_CHIPS * CORES, one, 0)

    def send_out(step):
        exchange(step, 1, send_ref, recv_ref, out_send, out_recv)

    def wait_for(ref, sem):
        pltpu.make_async_copy(ref, ref, sem).wait()

    def arrived_rows(step):
        return pl.ds(0, chunk - slots if step == 0 else chunk)

    def ring_copy(source, target, send_sem, recv_sem, direction):
        pltpu.make_async_remote_copy(
            src_ref=source,
            dst_ref=target,
            send_sem=send_sem,
            recv_sem=recv_sem,
            device_id=neighbour(direction),
            device_id_type=MESH,
        ).start()

    routes = [(matrix, direction) for matrix in range(2) for direction in range(2)]

    def sum_hop(step, matrix, direction, hop):
        offset = reach(matrix, direction) - hop + 1
        owner = ring_index(offset if direction == 0 else -offset)
        slot = hop_slot(matrix, direction, hop)
        if hop > 1:
            came = hop_slot(matrix, direction, hop - 1)
            wait_for(sums_ref.at[step, matrix, came], sum_recv.at[step, matrix, came])
            part_ref[step, matrix, owner] = (
                part_ref[step, matrix, owner].astype(jnp.float32)
                + sums_ref[step, matrix, came].astype(jnp.float32)
            ).astype(jnp.bfloat16)
        ring_copy(
            part_ref.at[step, matrix, owner],
            sums_ref.at[step, matrix, slot],
            sum_send,
            sum_recv.at[step, matrix, slot],
            direction,
        )

    def summed(step, matrix):
        value = part_ref[step, matrix, me_dp].astype(jnp.float32)
        for direction in range(2):
            came = hop_slot(matrix, direction, reach(matrix, direction))
            wait_for(sums_ref.at[step, matrix, came], sum_recv.at[step, matrix, came])
            value = value + sums_ref[step, matrix, came].astype(jnp.float32)
        return value

    def full_wait(step, matrix, direction, hop):
        owner = ring_index(-hop if direction == 0 else hop)
        came = hop_slot(matrix, direction, hop)
        wait_for(full_ref.at[step, matrix, owner], full_recv.at[step, matrix, came])

    def full_hop(step, matrix, direction, hop):
        offset = hop - 1
        owner = ring_index(-offset if direction == 0 else offset)
        if hop > 1:
            full_wait(step, matrix, direction, hop - 1)
        slot = hop_slot(matrix, direction, hop)
        ring_copy(
            full_ref.at[step, matrix, owner],
            full_ref.at[step, matrix, owner],
            full_send,
            full_recv.at[step, matrix, slot],
            direction,
        )

    def forward(step):
        wait_for(recv_ref.at[arrived_rows(step)], out_recv.at[step])
        if step == 0:
            load_up.wait()
            load_down.wait()
        for matrix in range(2):
            weight = up_ref if matrix == 0 else down_ref
            start = 0 if matrix == 0 else 2 * width - depth

            terms = matmul(recv_ref[chunk_rows(step), start : start + depth], weight[...])
            terms = terms.astype(jnp.bfloat16)
            for index in range(ring):
                part_ref[step, matrix, index] = terms[:, index * piece : (index + 1) * piece]
        for matrix, direction in routes:
            sum_hop(step, matrix, direction, 1)

    def turn(step):
        recv_turned[:, chunk_rows(step)] = recv_ref[chunk_rows(step), :].T

    def activate(step):
        preact = summed(step, 0)
        sigmoid = jax.nn.sigmoid(preact)
        full_ref[step, 0, me_dp] = (preact * sigmoid).astype(jnp.bfloat16)
        for direction in range(2):
            full_hop(step, 0, direction, 1)
        slope = sigmoid * (1.0 + preact * (1.0 - sigmoid))
        full_ref[step, 1, me_dp] = (summed(step, 1) * slope).astype(jnp.bfloat16)
        for direction in range(2):
            full_hop(step, 1, direction, 1)

    def backward(step):
        for direction in range(2):
            full_wait(step, 1, direction, reach(1, direction))
        act_cot = jnp.concatenate([full_ref[step, 1, index] for index in range(ring)], axis=1)
        rows = matmul(act_cot, up_ref[...], NT)
        back_ref[chunk_rows(step), :] = rows[:, :width].astype(jnp.bfloat16)
        if step == 0:
            own = pl.ds(pl.multiple_of(my_core * slots, slots), slots)
            returned_ref[own, :] = back_ref[own, :]
        exchange(step, -1, back_ref, returned_ref, back_send, back_recv)
        for direction in range(2):
            full_wait(step, 0, direction, reach(0, direction))

    def combine(step):
        wait_for(returned_ref.at[arrived_rows(step)], back_recv.at[step])
        rows = chunk_rows(step)
        terms = matmul(placing_ref[rows, :], returned_ref[rows, :], TN)
        combined_ref[...] = terms if step == 0 else combined_ref[...] + terms

    def weight_grads(step):
        def columns(block, carry):
            where = pl.ds(pl.multiple_of(block * 2 * piece, 2 * piece), 2 * piece)
            for matrix in range(2):
                rows = recv_turned[matrix * width : (matrix + 1) * width, chunk_rows(step)]
                pieces = [full_ref[step, 1 - matrix, 2 * block + half] for half in range(2)]
                terms = matmul(rows, jnp.concatenate(pieces, axis=1))
                if step > 0:
                    terms = terms + grad_sums_ref[matrix, :, where]
                if step < chunks - 1:
                    grad_sums_ref[matrix, :, where] = terms
                elif matrix == 0:
                    up_grad_ref[:, where] = terms.astype(jnp.bfloat16)
                else:
                    down_grad_ref[:, where] = terms.astype(jnp.bfloat16)
            return carry

        lax.fori_loop(0, ring // 2, columns, 0)

    place(0)
    pl.semaphore_wait(barrier, experts + 1)
    send_out(0)
    for step in range(1, chunks):
        place(step)
        send_out(step)

    def stage(step, number):
        if number == 0:
            forward(step)
        elif number < longest:
            for matrix, direction in routes:
                if number + 1 <= reach(matrix, direction):
                    sum_hop(step, matrix, direction, number + 1)
            if number == 1:
                turn(step)
        elif number == longest:
            activate(step)
        elif number < 2 * longest:
            for matrix, direction in routes:
                if number - longest + 1 <= reach(matrix, direction):
                    full_hop(step, matrix, direction, number - longest + 1)
        elif number == 2 * longest:
            backward(step)
        elif number == 2 * longest + 1:
            weight_grads(step)

    starts = STARTS[chunks]
    for tick in range(starts[-1] + 2 * longest + 2):
        for step in range(chunks):
            if 0 <= tick - starts[step] <= 2 * longest + 1:
                stage(step, tick - starts[step])

    store_up = pltpu.make_async_copy(up_grad_ref, up_grad_hbm, local_sem.at[0])
    store_down = pltpu.make_async_copy(down_grad_ref, down_grad_hbm, local_sem.at[1])
    store_up.start()
    store_down.start()
    for step in range(chunks):
        combine(step)
    token_grad_ref[...] = combined_ref[...].T.astype(jnp.bfloat16)

    moved = pl.ds(0, experts * slots - slots)
    wait_for(send_ref.at[moved], out_send)
    wait_for(back_ref.at[moved], back_send)
    wait_for(part_ref.at[:, :, pl.ds(0, ring - 1)], sum_send)
    wait_for(full_ref.at[:, :, pl.ds(0, ring - 1)], full_send)
    store_up.wait()
    store_down.wait()


def hand_over(*refs):
    for source, target in zip(refs[:3], refs[3:]):
        target[...] = source[...]


def per_device(
    chunks, z_chips, ring, tokens, cotangent, expert_ids, gate_levels, capacity, up_weight, down_weight
):
    tok_rows, width = tokens.shape
    experts = X_CHIPS * z_chips * CORES
    slots = tok_rows * expert_ids.shape[1] // experts
    rows = experts * slots
    chunk = rows // chunks
    hidden = up_weight.shape[2]
    piece = hidden // ring
    depth = -(-width // 128) * 128
    half = jnp.bfloat16
    vmem = pl.BlockSpec(memory_space=pltpu.VMEM)
    anywhere = pl.BlockSpec(memory_space=pl.ANY)
    dma = pltpu.SemaphoreType.DMA
    shapes = (
        jax.ShapeDtypeStruct((width, tok_rows), half),
        jax.ShapeDtypeStruct((width, hidden), half),
        jax.ShapeDtypeStruct((width, hidden), half),
    )
    results = pl.pallas_call(
        functools.partial(layer_kernel, chunks, z_chips, ring, slots),
        out_shape=shapes,
        in_specs=[vmem] * 5 + [anywhere] * 2,
        out_specs=(vmem, anywhere, anywhere),
        scratch_shapes=[
            pltpu.VMEM((rows, 2 * width), half),
            pltpu.VMEM((rows, 2 * width), half),
            pltpu.VMEM((2 * width, rows), half),
            pltpu.VMEM((rows, tok_rows), half),
            pltpu.VMEM((experts, tok_rows), half),
            pltpu.VMEM((experts, tok_rows), half),
            pltpu.VMEM((depth, hidden), half),
            pltpu.VMEM((depth, hidden), half),
            pltpu.VMEM((chunks, 2, ring, chunk, piece), half),
            pltpu.VMEM((chunks, 2, ring - 1, chunk, piece), half),
            pltpu.VMEM((chunks, 2, ring, chunk, piece), half),
            pltpu.VMEM((rows, width), half),
            pltpu.VMEM((rows, width), half),
            pltpu.VMEM((tok_rows, width), jnp.float32),
            pltpu.VMEM((2, width, hidden), jnp.float32),
            pltpu.VMEM((width, hidden), half),
            pltpu.VMEM((width, hidden), half),
            dma((2,)),
            dma,
            dma((chunks,)),
            dma,
            dma((chunks, 2, ring - 1)),
            dma,
            dma((chunks, 2, ring - 1)),
            dma,
            dma((chunks,)),
        ],
        compiler_params=pltpu.CompilerParams(
            collective_id=0, has_side_effects=True, vmem_limit_bytes=56 * 1024 * 1024
        ),
    )(
        tokens.T,
        cotangent.T,
        expert_ids.T,
        gate_levels.T,
        capacity.reshape(1, experts),
        up_weight[0],
        down_weight[0],
    )
    rows_of = [pl.BlockSpec((width // 4, out.shape[1]), lambda i: (i, 0)) for out in shapes]
    token_grad, up_grad, down_grad = pl.pallas_call(
        hand_over, out_shape=shapes, grid=(4,), in_specs=rows_of, out_specs=rows_of
    )(*results)
    return token_grad.T, up_grad[None], down_grad[None]


def solution(mesh):
    ring, experts = mesh.shape["dp"], mesh.shape["expert"]
    z_chips = experts // (X_CHIPS * CORES)
    return jax.shard_map(
        functools.partial(per_device, min(CHUNKS, z_chips), z_chips, ring),
        mesh=mesh,
        in_specs=(
            P("expert", "dp"),
            P("expert", "dp"),
            P("expert", None),
            P("expert", None),
            P(),
            P("expert", "dp", None),
            P("expert", "dp", None),
        ),
        out_specs=(P("expert", "dp"), P("expert", "dp", None), P("expert", "dp", None)),
        check_vma=False,
    )
```

```python
import functools

import jax
import jax.numpy as jnp
from jax import lax
from jax.experimental import pallas as pl
from jax.experimental.pallas import tpu as pltpu
from jax.sharding import PartitionSpec as P

MESH = pl.DeviceIdType.MESH
NN = (((1,), (0,)), ((), ()))
NT = (((1,), (1,)), ((), ()))
TN = (((0,), (0,)), ((), ()))
CHUNKS = 8
STARTS = {2: (0, 3), 4: (0, 4, 7, 9), 8: (0, 1, 2, 3, 5, 7, 8, 9)}
X_CHIPS, CORES = 4, 2
CHUNK_ORDER = {1: (0,), 2: (0, 1), 4: (0, 2, 3, 1), 8: (0, 1, 4, 6, 7, 5, 3, 2)}


def matmul(left, right, dims=NN):
    return lax.dot_general(left, right, dims, preferred_element_type=jnp.float32)


def layer_kernel(
    chunks,
    z_chips,
    ring,
    slots,
    tokens_ref,
    cot_ref,
    ids_ref,
    levels_ref,
    capacity_ref,
    up_hbm,
    down_hbm,
    token_grad_ref,
    up_grad_hbm,
    down_grad_hbm,
    send_ref,
    recv_ref,
    recv_turned,
    placing_ref,
    rank_ref,
    level_ref,
    up_ref,
    down_ref,
    part_ref,
    sums_ref,
    full_ref,
    back_ref,
    returned_ref,
    combined_ref,
    grad_sums_ref,
    up_grad_ref,
    down_grad_ref,
    local_sem,
    out_send,
    out_recv,
    sum_send,
    sum_recv,
    full_send,
    full_recv,
    back_send,
    back_recv,
):
    experts = X_CHIPS * z_chips * CORES
    width, tok_rows = tokens_ref.shape
    hidden = up_ref.shape[1]
    piece = hidden // ring
    depth = up_ref.shape[0]
    distances = z_chips // chunks
    layer = X_CHIPS * CORES * slots
    chunk = distances * layer
    top = ids_ref.shape[0]
    me_dp = lax.axis_index("dp")
    me = lax.axis_index("expert")
    my_core = lax.rem(me, CORES)
    my_z = lax.rem(lax.div(me, CORES), z_chips)
    my_x = lax.div(me, CORES * z_chips)
    after = lax.rem(me_dp + 1, ring)
    before = lax.rem(me_dp + ring - 1, ring)
    longest = ring // 2

    def distance(step, index):
        number = CHUNK_ORDER[chunks][step] * distances + index
        return (number + 1) // 2 * (1 if number % 2 else -1)

    def reach(matrix, direction):
        far = matrix == direction
        return longest if far else ring - 1 - longest

    def hop_slot(matrix, direction, hop):
        return (hop - 1) if direction == 0 else reach(matrix, 0) + hop - 1

    def neighbour(direction):
        return {"dp": after if direction == 0 else before}

    def ring_index(offset):
        return lax.rem(me_dp + offset + ring, ring)

    barrier = pltpu.get_barrier_semaphore()

    def greet(step, carry):
        pl.semaphore_signal(
            barrier,
            inc=1,
            device_id={"expert": lax.rem(me + step, experts)},
            device_id_type=MESH,
        )
        return carry

    lax.fori_loop(1, experts, greet, 0)
    for direction in range(2):
        pl.semaphore_signal(barrier, inc=1, device_id=neighbour(direction), device_id_type=MESH)

    up_rows = pl.ds(0, width)
    down_rows = pl.ds(depth - width, width)
    load_up = pltpu.make_async_copy(up_hbm, up_ref.at[up_rows], local_sem.at[0])
    load_down = pltpu.make_async_copy(down_hbm, down_ref.at[down_rows], local_sem.at[1])
    load_up.start()
    load_down.start()
    up_ref[pl.ds(width, depth - width), :] = jnp.zeros((depth - width, hidden), jnp.bfloat16)
    down_ref[pl.ds(0, depth - width), :] = jnp.zeros((depth - width, hidden), jnp.bfloat16)

    ids = ids_ref[...]
    levels = levels_ref[...]
    expert_row = lax.broadcasted_iota(jnp.int32, (experts, tok_rows), 0)
    named = jnp.zeros((experts, tok_rows), jnp.float32)
    level = jnp.zeros((experts, tok_rows), jnp.float32)
    for choice in range(top):
        hit = ids[choice : choice + 1, :] == expert_row
        named = named + jnp.where(hit, 1.0, 0.0)
        level = level + jnp.where(hit, levels[choice : choice + 1, :].astype(jnp.float32), 0.0)
    total = jnp.sum(levels.astype(jnp.float32), axis=0, keepdims=True)
    earlier = lax.broadcasted_iota(jnp.int32, (tok_rows, tok_rows), 0) < lax.broadcasted_iota(
        jnp.int32, (tok_rows, tok_rows), 1
    )
    rank = matmul(named.astype(jnp.bfloat16), jnp.where(earlier, 1.0, 0.0).astype(jnp.bfloat16))
    diagonal = lax.broadcasted_iota(jnp.int32, (experts, experts), 0) == lax.broadcasted_iota(
        jnp.int32, (experts, experts), 1
    )
    limit = jnp.sum(
        jnp.where(diagonal, capacity_ref[...].astype(jnp.float32), 0.0), axis=1, keepdims=True
    )
    kept = (named > 0.0) & (rank < limit)
    rank_ref[...] = jnp.where(kept, rank, -1.0).astype(jnp.bfloat16)
    level_ref[...] = level.astype(jnp.bfloat16)

    def chunk_rows(step):
        return pl.ds(step * chunk, chunk)

    def place(step):
        row = lax.broadcasted_iota(jnp.int32, (chunk, 1), 0)
        core = (row >> (slots.bit_length() - 1)) & (CORES - 1)
        x_away = (row >> ((CORES * slots).bit_length() - 1)) & (X_CHIPS - 1)
        z_away = jnp.zeros((chunk, 1), jnp.int32)
        for index in range(distances):
            here = (row >> (layer.bit_length() - 1)) == index
            z_away = jnp.where(here, distance(step, index), z_away)
        z_away = jnp.where((x_away & 1) == 1, -z_away, z_away)
        x_to = (my_x + x_away) & (X_CHIPS - 1)
        z_to = (my_z + z_away) & (z_chips - 1)
        expert = (x_to * z_chips + z_to) * CORES + core
        mine = expert == lax.broadcasted_iota(jnp.int32, (chunk, experts), 1)
        spread = jnp.where(mine, 1.0, 0.0).astype(jnp.bfloat16)
        slot = lax.broadcasted_iota(jnp.int32, (chunk, tok_rows), 0) & (slots - 1)
        matched = matmul(spread, rank_ref[...]) == slot.astype(jnp.float32)
        placing = jnp.where(matched, 1.0, 0.0)
        slot_level = jnp.sum(placing * matmul(spread, level_ref[...]), axis=1, keepdims=True)
        slot_total = jnp.sum(placing * total, axis=1, keepdims=True)
        gate = jnp.where(slot_total > 0.0, slot_level / jnp.maximum(slot_total, 1.0), 0.0)
        placing = placing.astype(jnp.bfloat16)
        placing_ref[chunk_rows(step), :] = placing
        both = jnp.concatenate([tokens_ref[...], cot_ref[...]], axis=0)
        rows = matmul(placing, both, NT)
        in_cot = lax.broadcasted_iota(jnp.int32, (chunk, 2 * width), 1) >= width
        rows = jnp.where(in_cot, gate * rows, rows)
        send_ref[chunk_rows(step), :] = rows.astype(jnp.bfloat16)
        if step == 0:
            own = pl.ds(pl.multiple_of(my_core * slots, slots), slots)
            recv_ref[own, :] = send_ref[own, :]

    def exchange(step, side, source, target, send_sem, recv_sem):
        for index in range(distances):
            base = step * chunk + index * layer

            def one(turn, carry, index=index, base=base):
                x_away = lax.div(turn, CORES)
                core = lax.rem(my_core + turn, CORES)
                z_away = distance(step, index) * (1 - 2 * lax.rem(x_away, 2))
                x_to = lax.rem(my_x + side * x_away + X_CHIPS, X_CHIPS)
                z_to = lax.rem(my_z + side * z_away + z_chips, z_chips)
                place_from = base + (x_away * CORES + core) * slots
                place_to = base + (x_away * CORES + my_core) * slots
                pltpu.make_async_remote_copy(
                    src_ref=source.at[pl.ds(pl.multiple_of(place_from, slots), slots)],
                    dst_ref=target.at[pl.ds(pl.multiple_of(place_to, slots), slots)],
                    send_sem=send_sem,
                    recv_sem=recv_sem.at[step],
                    device_id={"expert": (x_to * z_chips + z_to) * CORES + core},
                    device_id_type=MESH,
                ).start()
                return carry

            own = step == 0 and index == 0
            lax.fori_loop(1 if own else 0, X_CHIPS * CORES, one, 0)

    def send_out(step):
        exchange(step, 1, send_ref, recv_ref, out_send, out_recv)

    def wait_for(ref, sem):
        pltpu.make_async_copy(ref, ref, sem).wait()

    def arrived_rows(step):
        return pl.ds(0, chunk - slots if step == 0 else chunk)

    def ring_copy(source, target, send_sem, recv_sem, direction):
        pltpu.make_async_remote_copy(
            src_ref=source,
            dst_ref=target,
            send_sem=send_sem,
            recv_sem=recv_sem,
            device_id=neighbour(direction),
            device_id_type=MESH,
        ).start()

    routes = [(matrix, direction) for matrix in range(2) for direction in range(2)]

    def sum_hop(step, matrix, direction, hop):
        offset = reach(matrix, direction) - hop + 1
        owner = ring_index(offset if direction == 0 else -offset)
        slot = hop_slot(matrix, direction, hop)
        if hop > 1:
            came = hop_slot(matrix, direction, hop - 1)
            wait_for(sums_ref.at[step, matrix, came], sum_recv.at[step, matrix, came])
            part_ref[step, matrix, owner] = (
                part_ref[step, matrix, owner].astype(jnp.float32)
                + sums_ref[step, matrix, came].astype(jnp.float32)
            ).astype(jnp.bfloat16)
        ring_copy(
            part_ref.at[step, matrix, owner],
            sums_ref.at[step, matrix, slot],
            sum_send,
            sum_recv.at[step, matrix, slot],
            direction,
        )

    def summed(step, matrix):
        value = part_ref[step, matrix, me_dp].astype(jnp.float32)
        for direction in range(2):
            came = hop_slot(matrix, direction, reach(matrix, direction))
            wait_for(sums_ref.at[step, matrix, came], sum_recv.at[step, matrix, came])
            value = value + sums_ref[step, matrix, came].astype(jnp.float32)
        return value

    def full_wait(step, matrix, direction, hop):
        owner = ring_index(-hop if direction == 0 else hop)
        came = hop_slot(matrix, direction, hop)
        wait_for(full_ref.at[step, matrix, owner], full_recv.at[step, matrix, came])

    def full_hop(step, matrix, direction, hop):
        offset = hop - 1
        owner = ring_index(-offset if direction == 0 else offset)
        if hop > 1:
            full_wait(step, matrix, direction, hop - 1)
        slot = hop_slot(matrix, direction, hop)
        ring_copy(
            full_ref.at[step, matrix, owner],
            full_ref.at[step, matrix, owner],
            full_send,
            full_recv.at[step, matrix, slot],
            direction,
        )

    def forward(step):
        wait_for(recv_ref.at[arrived_rows(step)], out_recv.at[step])
        if step == 0:
            load_up.wait()
            load_down.wait()
        for matrix in range(2):
            weight = up_ref if matrix == 0 else down_ref
            start = 0 if matrix == 0 else 2 * width - depth

            terms = matmul(recv_ref[chunk_rows(step), start : start + depth], weight[...])
            terms = terms.astype(jnp.bfloat16)
            for index in range(ring):
                part_ref[step, matrix, index] = terms[:, index * piece : (index + 1) * piece]
        for matrix, direction in routes:
            sum_hop(step, matrix, direction, 1)

    def turn(step):
        recv_turned[:, chunk_rows(step)] = recv_ref[chunk_rows(step), :].T

    def activate(step):
        preact = summed(step, 0)
        sigmoid = jax.nn.sigmoid(preact)
        full_ref[step, 0, me_dp] = (preact * sigmoid).astype(jnp.bfloat16)
        for direction in range(2):
            full_hop(step, 0, direction, 1)
        slope = sigmoid * (1.0 + preact * (1.0 - sigmoid))
        full_ref[step, 1, me_dp] = (summed(step, 1) * slope).astype(jnp.bfloat16)
        for direction in range(2):
            full_hop(step, 1, direction, 1)

    def backward(step):
        for direction in range(2):
            full_wait(step, 1, direction, reach(1, direction))
        act_cot = jnp.concatenate([full_ref[step, 1, index] for index in range(ring)], axis=1)
        rows = matmul(act_cot, up_ref[...], NT)
        back_ref[chunk_rows(step), :] = rows[:, :width].astype(jnp.bfloat16)
        if step == 0:
            own = pl.ds(pl.multiple_of(my_core * slots, slots), slots)
            returned_ref[own, :] = back_ref[own, :]
        exchange(step, -1, back_ref, returned_ref, back_send, back_recv)
        for direction in range(2):
            full_wait(step, 0, direction, reach(0, direction))

    def combine(step):
        wait_for(returned_ref.at[arrived_rows(step)], back_recv.at[step])
        rows = chunk_rows(step)
        terms = matmul(placing_ref[rows, :], returned_ref[rows, :], TN)
        combined_ref[...] = terms if step == 0 else combined_ref[...] + terms

    def weight_grads(step):
        def columns(block, carry):
            where = pl.ds(pl.multiple_of(block * 2 * piece, 2 * piece), 2 * piece)
            for matrix in range(2):
                rows = recv_turned[matrix * width : (matrix + 1) * width, chunk_rows(step)]
                pieces = [full_ref[step, 1 - matrix, 2 * block + half] for half in range(2)]
                terms = matmul(rows, jnp.concatenate(pieces, axis=1))
                if step > 0:
                    terms = terms + grad_sums_ref[matrix, :, where]
                if step < chunks - 1:
                    grad_sums_ref[matrix, :, where] = terms
                elif matrix == 0:
                    up_grad_ref[:, where] = terms.astype(jnp.bfloat16)
                else:
                    down_grad_ref[:, where] = terms.astype(jnp.bfloat16)
            return carry

        lax.fori_loop(0, ring // 2, columns, 0)

    place(0)
    pl.semaphore_wait(barrier, experts + 1)
    send_out(0)
    for step in range(1, chunks):
        place(step)
        send_out(step)

    def stage(step, number):
        if number == 0:
            forward(step)
        elif number < longest:
            for matrix, direction in routes:
                if number + 1 <= reach(matrix, direction):
                    sum_hop(step, matrix, direction, number + 1)
            if number == 1:
                turn(step)
        elif number == longest:
            activate(step)
        elif number < 2 * longest:
            for matrix, direction in routes:
                if number - longest + 1 <= reach(matrix, direction):
                    full_hop(step, matrix, direction, number - longest + 1)
        elif number == 2 * longest:
            backward(step)
        elif number == 2 * longest + 1:
            weight_grads(step)

    starts = STARTS[chunks]
    for tick in range(starts[-1] + 2 * longest + 2):
        for step in range(chunks):
            if 0 <= tick - starts[step] <= 2 * longest + 1:
                stage(step, tick - starts[step])

    store_up = pltpu.make_async_copy(up_grad_ref, up_grad_hbm, local_sem.at[0])
    store_down = pltpu.make_async_copy(down_grad_ref, down_grad_hbm, local_sem.at[1])
    store_up.start()
    store_down.start()
    for step in range(chunks):
        combine(step)
    token_grad_ref[...] = combined_ref[...].T.astype(jnp.bfloat16)

    moved = pl.ds(0, experts * slots - slots)
    wait_for(send_ref.at[moved], out_send)
    wait_for(back_ref.at[moved], back_send)
    wait_for(part_ref.at[:, :, pl.ds(0, ring - 1)], sum_send)
    wait_for(full_ref.at[:, :, pl.ds(0, ring - 1)], full_send)
    store_up.wait()
    store_down.wait()


def hand_over(token_in, up_in, down_in, token_out, up_out, down_out, token, up, down, came, left):
    blocks = came.shape[1]
    rows = up.shape[0] // blocks
    steps = []
    for block in range(blocks):
        at = pl.ds(block * rows, rows)
        for index, (source, held, target) in enumerate(
            [(up_in, up, up_out), (down_in, down, down_out), (token_in, token, token_out)]
        ):
            load = pltpu.make_async_copy(source.at[at], held.at[at], came.at[index, block])
            store = pltpu.make_async_copy(held.at[at], target.at[at], left.at[index, block])
            steps.append((load, store))
    for load, store in steps:
        load.start()
    for load, store in steps:
        load.wait()
        store.start()
    for load, store in steps:
        store.wait()


def per_device(
    chunks, z_chips, ring, tokens, cotangent, expert_ids, gate_levels, capacity, up_weight, down_weight
):
    tok_rows, width = tokens.shape
    experts = X_CHIPS * z_chips * CORES
    slots = tok_rows * expert_ids.shape[1] // experts
    rows = experts * slots
    chunk = rows // chunks
    hidden = up_weight.shape[2]
    piece = hidden // ring
    depth = -(-width // 128) * 128
    half = jnp.bfloat16
    vmem = pl.BlockSpec(memory_space=pltpu.VMEM)
    anywhere = pl.BlockSpec(memory_space=pl.ANY)
    dma = pltpu.SemaphoreType.DMA
    shapes = (
        jax.ShapeDtypeStruct((width, tok_rows), half),
        jax.ShapeDtypeStruct((width, hidden), half),
        jax.ShapeDtypeStruct((width, hidden), half),
    )
    results = pl.pallas_call(
        functools.partial(layer_kernel, chunks, z_chips, ring, slots),
        out_shape=shapes,
        in_specs=[vmem] * 5 + [anywhere] * 2,
        out_specs=(vmem, anywhere, anywhere),
        scratch_shapes=[
            pltpu.VMEM((rows, 2 * width), half),
            pltpu.VMEM((rows, 2 * width), half),
            pltpu.VMEM((2 * width, rows), half),
            pltpu.VMEM((rows, tok_rows), half),
            pltpu.VMEM((experts, tok_rows), half),
            pltpu.VMEM((experts, tok_rows), half),
            pltpu.VMEM((depth, hidden), half),
            pltpu.VMEM((depth, hidden), half),
            pltpu.VMEM((chunks, 2, ring, chunk, piece), half),
            pltpu.VMEM((chunks, 2, ring - 1, chunk, piece), half),
            pltpu.VMEM((chunks, 2, ring, chunk, piece), half),
            pltpu.VMEM((rows, width), half),
            pltpu.VMEM((rows, width), half),
            pltpu.VMEM((tok_rows, width), jnp.float32),
            pltpu.VMEM((2, width, hidden), jnp.float32),
            pltpu.VMEM((width, hidden), half),
            pltpu.VMEM((width, hidden), half),
            dma((2,)),
            dma,
            dma((chunks,)),
            dma,
            dma((chunks, 2, ring - 1)),
            dma,
            dma((chunks, 2, ring - 1)),
            dma,
            dma((chunks,)),
        ],
        compiler_params=pltpu.CompilerParams(
            collective_id=0, has_side_effects=True, vmem_limit_bytes=56 * 1024 * 1024
        ),
    )(
        tokens.T,
        cotangent.T,
        expert_ids.T,
        gate_levels.T,
        capacity.reshape(1, experts),
        up_weight[0],
        down_weight[0],
    )
    token_grad, up_grad, down_grad = pl.pallas_call(
        hand_over,
        out_shape=shapes,
        in_specs=[anywhere] * 3,
        out_specs=(anywhere,) * 3,
        scratch_shapes=[pltpu.VMEM(out.shape, half) for out in shapes] + [dma((3, 2)), dma((3, 2))],
    )(*results)
    return token_grad.T, up_grad[None], down_grad[None]


def solution(mesh):
    ring, experts = mesh.shape["dp"], mesh.shape["expert"]
    z_chips = experts // (X_CHIPS * CORES)
    return jax.shard_map(
        functools.partial(per_device, min(CHUNKS, z_chips), z_chips, ring),
        mesh=mesh,
        in_specs=(
            P("expert", "dp"),
            P("expert", "dp"),
            P("expert", None),
            P("expert", None),
            P(),
            P("expert", "dp", None),
            P("expert", "dp", None),
        ),
        out_specs=(P("expert", "dp"), P("expert", "dp", None), P("expert", "dp", None)),
        check_vma=False,
    )
```

```python
import functools

import jax
import jax.numpy as jnp
from jax import lax
from jax.experimental import pallas as pl
from jax.experimental.pallas import tpu as pltpu
from jax.sharding import PartitionSpec as P

MESH = pl.DeviceIdType.MESH
NN = (((1,), (0,)), ((), ()))
NT = (((1,), (1,)), ((), ()))
TN = (((0,), (0,)), ((), ()))
CHUNKS = 8
STARTS = {2: (0, 3), 4: (0, 4, 7, 9), 8: (0, 1, 2, 3, 5, 7, 8, 9)}
X_CHIPS, CORES = 4, 2
CHUNK_ORDER = {1: (0,), 2: (0, 1), 4: (0, 2, 3, 1), 8: (0, 1, 4, 6, 7, 5, 3, 2)}


def matmul(left, right, dims=NN):
    return lax.dot_general(left, right, dims, preferred_element_type=jnp.float32)


def layer_kernel(
    chunks,
    z_chips,
    ring,
    slots,
    tokens_ref,
    cot_ref,
    ids_ref,
    levels_ref,
    capacity_ref,
    up_hbm,
    down_hbm,
    token_grad_ref,
    up_grad_hbm,
    down_grad_hbm,
    send_ref,
    recv_ref,
    recv_turned,
    placing_ref,
    rank_ref,
    level_ref,
    up_ref,
    down_ref,
    part_ref,
    sums_ref,
    full_ref,
    back_ref,
    returned_ref,
    combined_ref,
    grad_sums_ref,
    up_grad_ref,
    down_grad_ref,
    local_sem,
    out_send,
    out_recv,
    sum_send,
    sum_recv,
    full_send,
    full_recv,
    back_send,
    back_recv,
):
    experts = X_CHIPS * z_chips * CORES
    width, tok_rows = tokens_ref.shape
    hidden = up_ref.shape[1]
    piece = hidden // ring
    depth = up_ref.shape[0]
    distances = z_chips // chunks
    layer = X_CHIPS * CORES * slots
    chunk = distances * layer
    top = ids_ref.shape[0]
    me_dp = lax.axis_index("dp")
    me = lax.axis_index("expert")
    my_core = lax.rem(me, CORES)
    my_z = lax.rem(lax.div(me, CORES), z_chips)
    my_x = lax.div(me, CORES * z_chips)
    after = lax.rem(me_dp + 1, ring)
    before = lax.rem(me_dp + ring - 1, ring)
    longest = ring // 2

    def distance(step, index):
        number = CHUNK_ORDER[chunks][step] * distances + index
        return (number + 1) // 2 * (1 if number % 2 else -1)

    def reach(matrix, direction):
        far = matrix == direction
        return longest if far else ring - 1 - longest

    def hop_slot(matrix, direction, hop):
        return (hop - 1) if direction == 0 else reach(matrix, 0) + hop - 1

    def neighbour(direction):
        return {"dp": after if direction == 0 else before}

    def ring_index(offset):
        return lax.rem(me_dp + offset + ring, ring)

    barrier = pltpu.get_barrier_semaphore()

    def greet(step, carry):
        pl.semaphore_signal(
            barrier,
            inc=1,
            device_id={"expert": lax.rem(me + step, experts)},
            device_id_type=MESH,
        )
        return carry

    lax.fori_loop(1, experts, greet, 0)
    for direction in range(2):
        pl.semaphore_signal(barrier, inc=1, device_id=neighbour(direction), device_id_type=MESH)

    up_rows = pl.ds(0, width)
    down_rows = pl.ds(depth - width, width)
    load_up = pltpu.make_async_copy(up_hbm, up_ref.at[up_rows], local_sem.at[0])
    load_down = pltpu.make_async_copy(down_hbm, down_ref.at[down_rows], local_sem.at[1])
    load_up.start()
    load_down.start()
    up_ref[pl.ds(width, depth - width), :] = jnp.zeros((depth - width, hidden), jnp.bfloat16)
    down_ref[pl.ds(0, depth - width), :] = jnp.zeros((depth - width, hidden), jnp.bfloat16)

    ids = ids_ref[...]
    levels = levels_ref[...]
    expert_row = lax.broadcasted_iota(jnp.int32, (experts, tok_rows), 0)
    named = jnp.zeros((experts, tok_rows), jnp.float32)
    level = jnp.zeros((experts, tok_rows), jnp.float32)
    for choice in range(top):
        hit = ids[choice : choice + 1, :] == expert_row
        named = named + jnp.where(hit, 1.0, 0.0)
        level = level + jnp.where(hit, levels[choice : choice + 1, :].astype(jnp.float32), 0.0)
    total = jnp.sum(levels.astype(jnp.float32), axis=0, keepdims=True)
    earlier = lax.broadcasted_iota(jnp.int32, (tok_rows, tok_rows), 0) < lax.broadcasted_iota(
        jnp.int32, (tok_rows, tok_rows), 1
    )
    rank = matmul(named.astype(jnp.bfloat16), jnp.where(earlier, 1.0, 0.0).astype(jnp.bfloat16))
    diagonal = lax.broadcasted_iota(jnp.int32, (experts, experts), 0) == lax.broadcasted_iota(
        jnp.int32, (experts, experts), 1
    )
    limit = jnp.sum(
        jnp.where(diagonal, capacity_ref[...].astype(jnp.float32), 0.0), axis=1, keepdims=True
    )
    kept = (named > 0.0) & (rank < limit)
    rank_ref[...] = jnp.where(kept, rank, -1.0).astype(jnp.bfloat16)
    level_ref[...] = level.astype(jnp.bfloat16)

    def chunk_rows(step):
        return pl.ds(step * chunk, chunk)

    def place(step):
        row = lax.broadcasted_iota(jnp.int32, (chunk, 1), 0)
        core = (row >> (slots.bit_length() - 1)) & (CORES - 1)
        x_away = (row >> ((CORES * slots).bit_length() - 1)) & (X_CHIPS - 1)
        z_away = jnp.zeros((chunk, 1), jnp.int32)
        for index in range(distances):
            here = (row >> (layer.bit_length() - 1)) == index
            z_away = jnp.where(here, distance(step, index), z_away)
        z_away = jnp.where((x_away & 1) == 1, -z_away, z_away)
        x_to = (my_x + x_away) & (X_CHIPS - 1)
        z_to = (my_z + z_away) & (z_chips - 1)
        expert = (x_to * z_chips + z_to) * CORES + core
        mine = expert == lax.broadcasted_iota(jnp.int32, (chunk, experts), 1)
        spread = jnp.where(mine, 1.0, 0.0).astype(jnp.bfloat16)
        slot = lax.broadcasted_iota(jnp.int32, (chunk, tok_rows), 0) & (slots - 1)
        matched = matmul(spread, rank_ref[...]) == slot.astype(jnp.float32)
        placing = jnp.where(matched, 1.0, 0.0)
        slot_level = jnp.sum(placing * matmul(spread, level_ref[...]), axis=1, keepdims=True)
        slot_total = jnp.sum(placing * total, axis=1, keepdims=True)
        gate = jnp.where(slot_total > 0.0, slot_level / jnp.maximum(slot_total, 1.0), 0.0)
        placing = placing.astype(jnp.bfloat16)
        placing_ref[chunk_rows(step), :] = placing
        both = jnp.concatenate([tokens_ref[...], cot_ref[...]], axis=0)
        rows = matmul(placing, both, NT)
        in_cot = lax.broadcasted_iota(jnp.int32, (chunk, 2 * width), 1) >= width
        rows = jnp.where(in_cot, gate * rows, rows)
        send_ref[chunk_rows(step), :] = rows.astype(jnp.bfloat16)
        if step == 0:
            own = pl.ds(pl.multiple_of(my_core * slots, slots), slots)
            recv_ref[own, :] = send_ref[own, :]

    def exchange(step, side, source, target, send_sem, recv_sem):
        for index in range(distances):
            base = step * chunk + index * layer

            def one(turn, carry, index=index, base=base):
                x_away = lax.div(turn, CORES)
                core = lax.rem(my_core + turn, CORES)
                z_away = distance(step, index) * (1 - 2 * lax.rem(x_away, 2))
                x_to = lax.rem(my_x + side * x_away + X_CHIPS, X_CHIPS)
                z_to = lax.rem(my_z + side * z_away + z_chips, z_chips)
                place_from = base + (x_away * CORES + core) * slots
                place_to = base + (x_away * CORES + my_core) * slots
                pltpu.make_async_remote_copy(
                    src_ref=source.at[pl.ds(pl.multiple_of(place_from, slots), slots)],
                    dst_ref=target.at[pl.ds(pl.multiple_of(place_to, slots), slots)],
                    send_sem=send_sem,
                    recv_sem=recv_sem.at[step],
                    device_id={"expert": (x_to * z_chips + z_to) * CORES + core},
                    device_id_type=MESH,
                ).start()
                return carry

            own = step == 0 and index == 0
            lax.fori_loop(1 if own else 0, X_CHIPS * CORES, one, 0)

    def send_out(step):
        exchange(step, 1, send_ref, recv_ref, out_send, out_recv)

    def wait_for(ref, sem):
        pltpu.make_async_copy(ref, ref, sem).wait()

    def arrived_rows(step):
        return pl.ds(0, chunk - slots if step == 0 else chunk)

    def ring_copy(source, target, send_sem, recv_sem, direction):
        pltpu.make_async_remote_copy(
            src_ref=source,
            dst_ref=target,
            send_sem=send_sem,
            recv_sem=recv_sem,
            device_id=neighbour(direction),
            device_id_type=MESH,
        ).start()

    routes = [(0, 0), (1, 1), (1, 0), (0, 1)]

    def sum_hop(step, matrix, direction, hop):
        offset = reach(matrix, direction) - hop + 1
        owner = ring_index(offset if direction == 0 else -offset)
        slot = hop_slot(matrix, direction, hop)
        if hop > 1:
            came = hop_slot(matrix, direction, hop - 1)
            wait_for(sums_ref.at[step, matrix, came], sum_recv.at[step, matrix, came])
            part_ref[step, matrix, owner] = (
                part_ref[step, matrix, owner].astype(jnp.float32)
                + sums_ref[step, matrix, came].astype(jnp.float32)
            ).astype(jnp.bfloat16)
        ring_copy(
            part_ref.at[step, matrix, owner],
            sums_ref.at[step, matrix, slot],
            sum_send,
            sum_recv.at[step, matrix, slot],
            direction,
        )

    def summed(step, matrix):
        value = part_ref[step, matrix, me_dp].astype(jnp.float32)
        for direction in range(2):
            came = hop_slot(matrix, direction, reach(matrix, direction))
            wait_for(sums_ref.at[step, matrix, came], sum_recv.at[step, matrix, came])
            value = value + sums_ref[step, matrix, came].astype(jnp.float32)
        return value

    def full_wait(step, matrix, direction, hop):
        owner = ring_index(-hop if direction == 0 else hop)
        came = hop_slot(matrix, direction, hop)
        wait_for(full_ref.at[step, matrix, owner], full_recv.at[step, matrix, came])

    def full_hop(step, matrix, direction, hop):
        offset = hop - 1
        owner = ring_index(-offset if direction == 0 else offset)
        if hop > 1:
            full_wait(step, matrix, direction, hop - 1)
        slot = hop_slot(matrix, direction, hop)
        ring_copy(
            full_ref.at[step, matrix, owner],
            full_ref.at[step, matrix, owner],
            full_send,
            full_recv.at[step, matrix, slot],
            direction,
        )

    def forward(step):
        wait_for(recv_ref.at[arrived_rows(step)], out_recv.at[step])
        if step == 0:
            load_up.wait()
            load_down.wait()
        for matrix in range(2):
            weight = up_ref if matrix == 0 else down_ref
            start = 0 if matrix == 0 else 2 * width - depth

            terms = matmul(recv_ref[chunk_rows(step), start : start + depth], weight[...])
            terms = terms.astype(jnp.bfloat16)
            for index in range(ring):
                part_ref[step, matrix, index] = terms[:, index * piece : (index + 1) * piece]
        for matrix, direction in routes:
            sum_hop(step, matrix, direction, 1)

    def turn(step):
        recv_turned[:, chunk_rows(step)] = recv_ref[chunk_rows(step), :].T

    def activate(step):
        preact = summed(step, 0)
        sigmoid = jax.nn.sigmoid(preact)
        full_ref[step, 0, me_dp] = (preact * sigmoid).astype(jnp.bfloat16)
        for direction in range(2):
            full_hop(step, 0, direction, 1)
        slope = sigmoid * (1.0 + preact * (1.0 - sigmoid))
        full_ref[step, 1, me_dp] = (summed(step, 1) * slope).astype(jnp.bfloat16)
        for direction in range(2):
            full_hop(step, 1, direction, 1)

    def backward(step):
        for direction in range(2):
            full_wait(step, 1, direction, reach(1, direction))
        act_cot = jnp.concatenate([full_ref[step, 1, index] for index in range(ring)], axis=1)
        rows = matmul(act_cot, up_ref[...], NT)
        back_ref[chunk_rows(step), :] = rows[:, :width].astype(jnp.bfloat16)
        if step == 0:
            own = pl.ds(pl.multiple_of(my_core * slots, slots), slots)
            returned_ref[own, :] = back_ref[own, :]
        exchange(step, -1, back_ref, returned_ref, back_send, back_recv)
        for direction in range(2):
            full_wait(step, 0, direction, reach(0, direction))

    def combine(step):
        wait_for(returned_ref.at[arrived_rows(step)], back_recv.at[step])
        rows = chunk_rows(step)
        terms = matmul(placing_ref[rows, :], returned_ref[rows, :], TN)
        combined_ref[...] = terms if step == 0 else combined_ref[...] + terms

    def weight_grads(step):
        def columns(block, carry):
            where = pl.ds(pl.multiple_of(block * 2 * piece, 2 * piece), 2 * piece)
            for matrix in range(2):
                rows = recv_turned[matrix * width : (matrix + 1) * width, chunk_rows(step)]
                pieces = [full_ref[step, 1 - matrix, 2 * block + half] for half in range(2)]
                terms = matmul(rows, jnp.concatenate(pieces, axis=1))
                if step > 0:
                    terms = terms + grad_sums_ref[matrix, :, where]
                if step < chunks - 1:
                    grad_sums_ref[matrix, :, where] = terms
                elif matrix == 0:
                    up_grad_ref[:, where] = terms.astype(jnp.bfloat16)
                else:
                    down_grad_ref[:, where] = terms.astype(jnp.bfloat16)
            return carry

        lax.fori_loop(0, ring // 2, columns, 0)

    place(0)
    pl.semaphore_wait(barrier, experts + 1)
    send_out(0)
    for step in range(1, chunks):
        place(step)
        send_out(step)

    def stage(step, number):
        if number == 0:
            forward(step)
        elif number < longest:
            for matrix, direction in routes:
                if number + 1 <= reach(matrix, direction):
                    sum_hop(step, matrix, direction, number + 1)
            if number == 1:
                turn(step)
        elif number == longest:
            activate(step)
        elif number < 2 * longest:
            for matrix, direction in routes:
                if number - longest + 1 <= reach(matrix, direction):
                    full_hop(step, matrix, direction, number - longest + 1)
        elif number == 2 * longest:
            backward(step)
        elif number == 2 * longest + 1:
            weight_grads(step)

    starts = STARTS[chunks]
    for tick in range(starts[-1] + 2 * longest + 2):
        for step in range(chunks):
            if 0 <= tick - starts[step] <= 2 * longest + 1:
                stage(step, tick - starts[step])

    store_up = pltpu.make_async_copy(up_grad_ref, up_grad_hbm, local_sem.at[0])
    store_down = pltpu.make_async_copy(down_grad_ref, down_grad_hbm, local_sem.at[1])
    store_up.start()
    store_down.start()
    for step in range(chunks):
        combine(step)
    token_grad_ref[...] = combined_ref[...].T.astype(jnp.bfloat16)

    moved = pl.ds(0, experts * slots - slots)
    wait_for(send_ref.at[moved], out_send)
    wait_for(back_ref.at[moved], back_send)
    wait_for(part_ref.at[:, :, pl.ds(0, ring - 1)], sum_send)
    wait_for(full_ref.at[:, :, pl.ds(0, ring - 1)], full_send)
    store_up.wait()
    store_down.wait()


def hand_over(token_in, up_in, down_in, token_out, up_out, down_out, token, up, down, came, left):
    blocks = came.shape[1]
    rows = up.shape[0] // blocks
    steps = []
    for block in range(blocks):
        at = pl.ds(block * rows, rows)
        for index, (source, held, target) in enumerate(
            [(up_in, up, up_out), (down_in, down, down_out), (token_in, token, token_out)]
        ):
            load = pltpu.make_async_copy(source.at[at], held.at[at], came.at[index, block])
            store = pltpu.make_async_copy(held.at[at], target.at[at], left.at[index, block])
            steps.append((load, store))
    for load, store in steps:
        load.start()
    for load, store in steps:
        load.wait()
        store.start()
    for load, store in steps:
        store.wait()


def per_device(
    chunks, z_chips, ring, tokens, cotangent, expert_ids, gate_levels, capacity, up_weight, down_weight
):
    tok_rows, width = tokens.shape
    experts = X_CHIPS * z_chips * CORES
    slots = tok_rows * expert_ids.shape[1] // experts
    rows = experts * slots
    chunk = rows // chunks
    hidden = up_weight.shape[2]
    piece = hidden // ring
    depth = -(-width // 128) * 128
    half = jnp.bfloat16
    vmem = pl.BlockSpec(memory_space=pltpu.VMEM)
    anywhere = pl.BlockSpec(memory_space=pl.ANY)
    dma = pltpu.SemaphoreType.DMA
    shapes = (
        jax.ShapeDtypeStruct((width, tok_rows), half),
        jax.ShapeDtypeStruct((width, hidden), half),
        jax.ShapeDtypeStruct((width, hidden), half),
    )
    results = pl.pallas_call(
        functools.partial(layer_kernel, chunks, z_chips, ring, slots),
        out_shape=shapes,
        in_specs=[vmem] * 5 + [anywhere] * 2,
        out_specs=(vmem, anywhere, anywhere),
        scratch_shapes=[
            pltpu.VMEM((rows, 2 * width), half),
            pltpu.VMEM((rows, 2 * width), half),
            pltpu.VMEM((2 * width, rows), half),
            pltpu.VMEM((rows, tok_rows), half),
            pltpu.VMEM((experts, tok_rows), half),
            pltpu.VMEM((experts, tok_rows), half),
            pltpu.VMEM((depth, hidden), half),
            pltpu.VMEM((depth, hidden), half),
            pltpu.VMEM((chunks, 2, ring, chunk, piece), half),
            pltpu.VMEM((chunks, 2, ring - 1, chunk, piece), half),
            pltpu.VMEM((chunks, 2, ring, chunk, piece), half),
            pltpu.VMEM((rows, width), half),
            pltpu.VMEM((rows, width), half),
            pltpu.VMEM((tok_rows, width), jnp.float32),
            pltpu.VMEM((2, width, hidden), jnp.float32),
            pltpu.VMEM((width, hidden), half),
            pltpu.VMEM((width, hidden), half),
            dma((2,)),
            dma,
            dma((chunks,)),
            dma,
            dma((chunks, 2, ring - 1)),
            dma,
            dma((chunks, 2, ring - 1)),
            dma,
            dma((chunks,)),
        ],
        compiler_params=pltpu.CompilerParams(
            collective_id=0, has_side_effects=True, vmem_limit_bytes=56 * 1024 * 1024
        ),
    )(
        tokens.T,
        cotangent.T,
        expert_ids.T,
        gate_levels.T,
        capacity.reshape(1, experts),
        up_weight[0],
        down_weight[0],
    )
    token_grad, up_grad, down_grad = pl.pallas_call(
        hand_over,
        out_shape=shapes,
        in_specs=[anywhere] * 3,
        out_specs=(anywhere,) * 3,
        scratch_shapes=[pltpu.VMEM(out.shape, half) for out in shapes] + [dma((3, 2)), dma((3, 2))],
    )(*results)
    return token_grad.T, up_grad[None], down_grad[None]


def solution(mesh):
    ring, experts = mesh.shape["dp"], mesh.shape["expert"]
    z_chips = experts // (X_CHIPS * CORES)
    return jax.shard_map(
        functools.partial(per_device, min(CHUNKS, z_chips), z_chips, ring),
        mesh=mesh,
        in_specs=(
            P("expert", "dp"),
            P("expert", "dp"),
            P("expert", None),
            P("expert", None),
            P(),
            P("expert", "dp", None),
            P("expert", "dp", None),
        ),
        out_specs=(P("expert", "dp"), P("expert", "dp", None), P("expert", "dp", None)),
        check_vma=False,
    )
```
